512 devices in a mesh: pair: 64 (over z_hi, y, core), tm: 8 (over x, z_lo).
Axes of the slice: x: 4, y: 8, z: 8 (z_hi: 4, z_lo: 2; z = z_hi * 2 + z_lo), core: 2. Of those that a mesh axis runs over, the one named last changes fastest.
Arguments:
- raw: bfloat16 [8, 16384, 128], P('tm', 'pair'), may hold values from -60 to 60
- valid: int32 [8, 16384], P('tm', 'pair'), may hold values 0 or 1
Outputs:
- near_corr: float32 [16384, 4096], P('pair', 'tm')
- far_corr: float32 [16384, 4096], P('pair', 'tm')
The draws below stay inside these ranges and needn't reach their ends.
All inputs are finite; a program needn't handle non-finite values. No bound on the sum of `valid` on one device may be relied on, other than what follows from the above.
Results may differ from the reference program's by a relative error of at most 0.014.
Values may be sent and summed in bfloat16 or wider, within the bound.
No kernel may reach another device: no remote copies, remote signals or barrier semaphores. Data moves between devices by JAX's collectives and lax.ppermute only.
A program may use at most 64 MiB of HBM per device.

```python
import math
import jax
import jax.numpy as jnp
from jax import lax

W_DEV = 1
CB = 256
F = 64
LAGS = 16
NT = 128
WINDOWS = 8
CHANNELS = 16384
N_PAIR = 64


def draw_raw(key, part):
    key_base, key_amp = jax.random.split(key, 2)
    shape = (WINDOWS, CHANNELS, NT)
    amplitude = jnp.exp(jax.random.uniform(key_amp, shape, jnp.float32, 0.0, math.log(10.0)))
    values = jax.random.normal(key_base, shape, jnp.float32) * amplitude
    return jnp.clip(values, -60.0, 60.0).astype(jnp.bfloat16)


def plant(drawn, rng, smallest, largest):
    dims = drawn.shape
    spot = [jax.random.randint(jax.random.fold_in(rng, axis), (), 0, dims[axis]) for axis in range(len(dims))]
    drawn = drawn.at[tuple(spot)].set(smallest)
    longest = dims.index(max(dims))
    spot[longest] = (spot[longest] + 1) % dims[longest]
    return drawn.at[tuple(spot)].set(largest)


def setup_inputs(seed: int = 0) -> dict:
    seeds = jax.random.split(jax.random.key(seed), 3)
    return {
        "raw": draw_raw(jax.random.fold_in(seeds[2], 71), 0),
        "valid": plant((jax.random.randint(seeds[1], (WINDOWS, CHANNELS), 0, 8) < 7).astype(jnp.int32), jax.random.fold_in(seeds[1], 1), 0, 1),
    }


def make_basis(samples, freqs):
    times = jnp.arange(samples, dtype=jnp.float32)[:, None]
    bins = jnp.arange(freqs, dtype=jnp.float32)[None, :]
    hann = 0.5 - 0.5 * jnp.cos(2.0 * math.pi * times / samples)
    angle = 2.0 * math.pi * bins * times / samples
    return jnp.concatenate([hann * jnp.cos(angle), -hann * jnp.sin(angle)], axis=1).astype(jnp.bfloat16)

def lag_tables(lags, freqs, samples):
    shift_lag = jnp.arange(lags, dtype=jnp.float32)[:, None] - lags // 2
    bins = jnp.arange(freqs, dtype=jnp.float32)[None, :]
    theta = 2.0 * math.pi * bins * shift_lag / samples
    return (jnp.cos(theta).astype(jnp.bfloat16), jnp.sin(theta).astype(jnp.bfloat16))

def whiten_block(block_raw, block_valid, basis):
    windows, chans, samples = block_raw.shape
    spectra = jnp.dot(block_raw.reshape(windows * chans, samples), basis, preferred_element_type=jnp.float32)
    spectra = spectra.reshape(windows, chans, basis.shape[1])
    power = lax.optimization_barrier(jnp.mean(spectra * spectra, axis=-1, keepdims=True)) + 1e-06
    return (spectra * lax.rsqrt(power) * block_valid[..., None].astype(jnp.float32)).astype(jnp.bfloat16)

def modulate(other, cos_wide, sin_wide, freqs):
    oth_re = jnp.transpose(other[:, :, :freqs], (0, 2, 1)).astype(jnp.float32)[:, :, None, :]
    oth_im = jnp.transpose(other[:, :, freqs:], (0, 2, 1)).astype(jnp.float32)[:, :, None, :]
    mod_a = cos_wide * oth_re + sin_wide * oth_im
    mod_b = cos_wide * oth_im - sin_wide * oth_re
    return jnp.stack([mod_a, mod_b], axis=1).astype(jnp.bfloat16)

def reference(raw, valid):
    basis = make_basis(NT, F)
    cos_table, sin_table = lag_tables(LAGS, F, NT)
    cos_wide = jnp.transpose(cos_table.astype(jnp.float32))[None, :, :, None]
    sin_wide = jnp.transpose(sin_table.astype(jnp.float32))[None, :, :, None]
    blocks_raw = jnp.transpose(raw.reshape(WINDOWS, N_PAIR, CB, NT), (1, 0, 2, 3))
    blocks_valid = jnp.transpose(valid.reshape(WINDOWS, N_PAIR, CB), (1, 0, 2))
    white_all = lax.map(lambda pair_in: whiten_block(pair_in[0], pair_in[1], basis), (blocks_raw, blocks_valid))
    scale = 1.0 / math.sqrt(WINDOWS * F)
    groups = WINDOWS // W_DEV

    def round_corr(offset):

        def one_block(index):
            own = white_all[index].reshape(groups, W_DEV, CB, 2 * F)
            other = white_all[((index + offset) % N_PAIR).astype(jnp.int32)].reshape(groups, W_DEV, CB, 2 * F)

            def one_group(pieces):
                mod = modulate(pieces[1], cos_wide, sin_wide, F).reshape(W_DEV * 2 * F, LAGS * CB)
                left = jnp.transpose(pieces[0], (1, 0, 2)).reshape(CB, W_DEV * 2 * F)
                corr = jnp.dot(left, mod, preferred_element_type=jnp.float32)
                return (corr * scale).astype(jnp.bfloat16).astype(jnp.float32)
            partials = lax.map(one_group, (own, other))
            return lax.optimization_barrier(jnp.sum(partials, axis=0))
        result = lax.map(one_block, jnp.arange(N_PAIR, dtype=jnp.int32))
        return result.reshape(CHANNELS, LAGS * CB)
    return (round_corr(1), round_corr(2))
```

```python
import math

import jax
import jax.numpy as jnp
from jax import lax
from jax.experimental import pallas as pl
from jax.experimental.pallas import tpu as pltpu
from jax.sharding import PartitionSpec as P

LAGS = 16


def make_basis(samples, freqs):
    times = jnp.arange(samples, dtype=jnp.float32)[:, None]
    bins = jnp.arange(freqs, dtype=jnp.float32)[None, :]
    hann = 0.5 - 0.5 * jnp.cos(2.0 * math.pi * times / samples)
    angle = 2.0 * math.pi * bins * times / samples
    return jnp.concatenate([hann * jnp.cos(angle), -hann * jnp.sin(angle)], axis=1).astype(
        jnp.bfloat16
    )


def lag_tables(first, lags, freqs, samples):
    shift_lag = (first + jnp.arange(lags) - LAGS // 2).astype(jnp.float32)[:, None]
    bins = jnp.arange(freqs, dtype=jnp.float32)[None, :]
    theta = 2.0 * math.pi * bins * shift_lag / samples
    cos = jnp.cos(theta).astype(jnp.bfloat16).astype(jnp.float32)
    sin = jnp.sin(theta).astype(jnp.bfloat16).astype(jnp.float32)
    return jnp.concatenate([cos, cos], axis=1), jnp.concatenate([-sin, sin], axis=1)


def in_vmem(value):
    return pltpu.with_memory_space_constraint(value, pltpu.VMEM)


def rotated(own, cos, sin):
    wide = own.astype(jnp.float32)
    swapped = pltpu.roll(wide, wide.shape[-1] // 2, 1)
    return (wide * cos + swapped * sin).astype(jnp.bfloat16)


def far_kernel(odd_ref, gath_ref, cos_ref, sin_ref, out_ref, mod_ref, *, scale):
    windows, both, width = gath_ref.shape
    chans = both // 2
    lag = pl.program_id(0)
    odd = odd_ref[0]
    own_at = pl.multiple_of(odd * chans, chans)
    far_at = pl.multiple_of((1 - odd) * chans, chans)
    rows = pl.multiple_of(lag * chans, chans)
    cos = cos_ref[pl.ds(lag, 1), :]
    sin = sin_ref[pl.ds(lag, 1), :]
    for w in range(windows):
        own = gath_ref[w, pl.ds(own_at, chans), :]
        mod_ref[pl.ds(rows, chans), w * width : (w + 1) * width] = rotated(own, cos, sin)
    other = jnp.concatenate(
        [gath_ref[w, pl.ds(far_at, chans), :] for w in range(windows)], axis=1
    )
    total = lax.dot_general(
        mod_ref[pl.ds(rows, chans), :], other, (((1,), (1,)), ((), ())), preferred_element_type=jnp.float32
    )
    out_ref[...] = total * scale


def near_kernel(mod_ref, other_ref, out_ref, *, scale):
    windows, chans, _ = other_ref.shape
    lag = pl.program_id(0)
    other = jnp.concatenate([other_ref[w] for w in range(windows)], axis=1)
    rows = pl.multiple_of(lag * chans, chans)
    total = lax.dot_general(
        mod_ref[pl.ds(rows, chans), :], other, (((1,), (1,)), ((), ())), preferred_element_type=jnp.float32
    )
    out_ref[...] = total * scale


def local(raw, valid):
    windows, chans, samples = raw.shape
    freqs = samples // 2
    groups = lax.axis_size("tm")
    pairs = lax.axis_size("pair")
    total = windows * groups
    lags = LAGS // groups
    scale = 1.0 / math.sqrt(total * freqs)
    basis = make_basis(samples, freqs)
    cos, sin = lag_tables(lax.axis_index("tm") * lags, lags, freqs, samples)
    odd = (lax.axis_index("pair") % 2).astype(jnp.int32)
    spectra = jnp.dot(
        raw.reshape(windows * chans, samples), basis, preferred_element_type=jnp.float32
    )
    spectra = spectra.reshape(windows, chans, 2 * freqs)
    power = jnp.mean(spectra * spectra, axis=-1, keepdims=True) + 1e-06
    white = (spectra * lax.rsqrt(power) * valid[..., None].astype(jnp.float32)).astype(jnp.bfloat16)

    far = lax.ppermute(white, "pair", [(p, (p - 2) % pairs) for p in range(pairs)])
    is_odd = odd == 1
    slots = jnp.concatenate([jnp.where(is_odd, far, white), jnp.where(is_odd, white, far)], axis=1)
    sends = jnp.broadcast_to(slots[None], (groups, windows, 2 * chans, samples))
    gathered = lax.all_to_all(
        sends.reshape(total, 2 * chans, samples), "tm", 0, 0, tiled=True
    )
    near = lax.ppermute(gathered[:, chans:, :], "pair", [(p, p ^ 1) for p in range(pairs)])

    vmem = pl.BlockSpec(memory_space=pltpu.VMEM)
    far_corr, mod = pl.pallas_call(
        lambda *refs: far_kernel(*refs, scale=scale),
        grid=(lags,),
        in_specs=[
            pl.BlockSpec(memory_space=pltpu.SMEM),
            vmem,
            vmem,
            vmem,
        ],
        out_specs=[
            pl.BlockSpec((chans, chans), lambda l: (0, l)),
            vmem,
        ],
        out_shape=[
            jax.ShapeDtypeStruct((chans, lags * chans), jnp.float32),
            pltpu.VMEM((lags * chans, total * samples), jnp.bfloat16),
        ],
        name="far_corr",
    )(odd.reshape(1), in_vmem(gathered), in_vmem(cos), in_vmem(sin))
    near_corr = pl.pallas_call(
        lambda *refs: near_kernel(*refs, scale=scale),
        grid=(lags,),
        in_specs=[
            vmem,
            vmem,
        ],
        out_specs=pl.BlockSpec((chans, chans), lambda l: (0, l)),
        out_shape=jax.ShapeDtypeStruct((chans, lags * chans), jnp.float32),
        name="near_corr",
    )(mod, in_vmem(near))
    return (near_corr, far_corr)


def solution(mesh):
    return jax.shard_map(
        local,
        mesh=mesh,
        in_specs=(P("tm", "pair", None), P("tm", "pair")),
        out_specs=(P("pair", "tm"), P("pair", "tm")),
        check_vma=False,
    )
```

```python
import functools
import math

import jax
import jax.numpy as jnp
import numpy as np
from jax import lax
from jax.experimental import pallas as pl
from jax.experimental.pallas import tpu as pltpu
from jax.sharding import PartitionSpec as P

LAGS = 16


def make_basis(samples, freqs):
    times = np.arange(samples, dtype=np.float64)[:, None]
    bins = np.arange(freqs, dtype=np.float64)[None, :]
    hann = 0.5 - 0.5 * np.cos(2.0 * math.pi * times / samples)
    angle = 2.0 * math.pi * bins * times / samples
    return np.concatenate([hann * np.cos(angle), -hann * np.sin(angle)], axis=1).astype(
        jnp.bfloat16
    )


def lag_tables(lags, freqs, samples):
    shift_lag = np.arange(lags, dtype=np.float64)[:, None] - lags // 2
    bins = np.arange(freqs, dtype=np.float64)[None, :]
    theta = 2.0 * math.pi * bins * shift_lag / samples
    cos = np.cos(theta).astype(jnp.bfloat16).astype(np.float32)
    sin = np.sin(theta).astype(jnp.bfloat16).astype(np.float32)
    return np.concatenate([cos, cos, -sin, sin], axis=1)


def in_vmem(value):
    return pltpu.with_memory_space_constraint(value, pltpu.VMEM)


VMEM_SPEC = pl.BlockSpec(memory_space=pltpu.VMEM)


def on_chip(kernel, name, out, *args, scalars=()):
    return pl.pallas_call(
        kernel,
        in_specs=[pl.BlockSpec(memory_space=pltpu.SMEM)] * len(scalars) + [VMEM_SPEC] * len(args),
        out_specs=jax.tree.map(lambda _: VMEM_SPEC, out),
        out_shape=out,
        name=name,
    )(*[jnp.reshape(scalar, (1,)) for scalar in scalars], *[in_vmem(arg) for arg in args])


def whiten_kernel(raw_hbm, valid_hbm, basis_hbm, white_ref, send_ref, raw_ref, valid_ref, basis_ref, sems):
    pairs = ((raw_hbm, raw_ref), (basis_hbm, basis_ref), (valid_hbm, valid_ref))
    loads = [pltpu.make_async_copy(src, dst, sems.at[i]) for i, (src, dst) in enumerate(pairs)]
    for load in loads:
        load.start()
    for load in loads:
        load.wait()
    chans, width = white_ref.shape[1:]
    spectra = jnp.dot(raw_ref[0], basis_ref[...], preferred_element_type=jnp.float32)
    power = jnp.mean(spectra * spectra, axis=-1, keepdims=True) + 1e-06
    mask = jnp.transpose(jnp.broadcast_to(valid_ref[...].astype(jnp.float32), (width, chans)))
    white = (spectra * lax.rsqrt(power) * mask).astype(jnp.bfloat16)
    white_ref[0] = white
    for peer in range(send_ref.shape[0]):
        send_ref[peer] = white


def whiten(raw, valid, basis, out):
    anywhere = pl.BlockSpec(memory_space=pl.ANY)
    return pl.pallas_call(
        whiten_kernel,
        in_specs=[anywhere] * 3,
        out_specs=jax.tree.map(lambda _: VMEM_SPEC, out),
        out_shape=out,
        scratch_shapes=[
            pltpu.VMEM(raw.shape, raw.dtype),
            pltpu.VMEM(valid.shape, valid.dtype),
            pltpu.VMEM(basis.shape, basis.dtype),
            pltpu.SemaphoreType.DMA((3,)),
        ],
        name="whiten",
    )(raw, valid, basis)


def spread_kernel(block_ref, send_ref):
    for peer in range(send_ref.shape[0]):
        send_ref[peer] = block_ref[0]


def rotate_kernel(slot_ref, own_ref, table_ref, mod_ref):
    windows, chans, width = own_ref.shape
    lags = mod_ref.shape[0] // chans
    for lag in range(lags):
        turn = table_ref[pl.ds(slot_ref[0] * lags + lag, 1), :]
        cos, sin = turn[:, :width], turn[:, width:]
        for w in range(windows):
            own = own_ref[w].astype(jnp.float32)
            turned = own * cos + pltpu.roll(own, width // 2, 1) * sin
            mod_ref[lag * chans : (lag + 1) * chans, w * width : (w + 1) * width] = turned.astype(
                jnp.bfloat16
            )


def choose_kernel(odd_ref, own_ref, far_ref, out_ref):
    @pl.when(odd_ref[0] == 1)
    def _():
        out_ref[...] = own_ref[...]

    @pl.when(odd_ref[0] == 0)
    def _():
        out_ref[...] = far_ref[...]


def corr_kernel(mod_ref, other_ref, out_ref, *, scale):
    windows, chans, _ = other_ref.shape
    rows = pl.multiple_of(pl.program_id(0) * chans, chans)
    other = jnp.concatenate([other_ref[w] for w in range(windows)], axis=1)
    total = lax.dot_general(
        mod_ref[pl.ds(rows, chans), :],
        other,
        (((1,), (1,)), ((), ())),
        preferred_element_type=jnp.float32,
    )
    out_ref[...] = total * scale


def correlate(mod, other, lags, scale, name):
    chans = other.shape[1]
    return pl.pallas_call(
        functools.partial(corr_kernel, scale=scale),
        grid=(lags,),
        in_specs=[VMEM_SPEC, VMEM_SPEC],
        out_specs=pl.BlockSpec((chans, chans), lambda lag: (0, lag)),
        out_shape=jax.ShapeDtypeStruct((chans, lags * chans), jnp.float32),
        name=name,
    )(in_vmem(mod), in_vmem(other))


def local(raw, valid):
    windows, chans, samples = raw.shape
    freqs = samples // 2
    groups = lax.axis_size("tm")
    pairs = lax.axis_size("pair")
    total = windows * groups
    lags = LAGS // groups
    scale = 1.0 / math.sqrt(total * freqs)
    slot = lax.axis_index("tm")
    odd = lax.axis_index("pair") & 1
    basis = jnp.asarray(make_basis(samples, freqs))
    table = jnp.asarray(lag_tables(LAGS, freqs, samples))
    spread = pltpu.VMEM((total, chans, samples), jnp.bfloat16)
    white, own_sends = whiten(
        raw, valid, basis, (pltpu.VMEM((windows, chans, samples), jnp.bfloat16), spread)
    )
    own = lax.all_to_all(own_sends, "tm", 0, 0, tiled=True)
    far_white = lax.ppermute(white, "pair", [(p, (p - 2) % pairs) for p in range(pairs)])
    far_sends = on_chip(spread_kernel, "spread", spread, far_white)
    far = lax.all_to_all(far_sends, "tm", 0, 0, tiled=True)
    mod = on_chip(
        rotate_kernel,
        "rotate",
        pltpu.VMEM((lags * chans, total * samples), jnp.bfloat16),
        own,
        table,
        scalars=(slot,),
    )
    swap = on_chip(choose_kernel, "choose", spread, own, far, scalars=(odd,))
    swap, mod = lax.optimization_barrier((swap, mod))
    near = lax.ppermute(swap, "pair", [(p, p ^ 1) for p in range(pairs)])
    far_corr = correlate(mod, far, lags, scale, "far_corr")
    near_corr = correlate(mod, near, lags, scale, "near_corr")
    return (near_corr, far_corr)


def solution(mesh):
    return jax.shard_map(
        local,
        mesh=mesh,
        in_specs=(P("tm", "pair", None), P("tm", "pair")),
        out_specs=(P("pair", "tm"), P("pair", "tm")),
        check_vma=False,
    )
```

```python
import functools
import math

import jax
import jax.numpy as jnp
import numpy as np
from jax import lax
from jax.experimental import pallas as pl
from jax.experimental.pallas import tpu as pltpu
from jax.sharding import PartitionSpec as P

LAGS = 16


def make_basis(samples, freqs):
    times = np.arange(samples, dtype=np.float64)[:, None]
    bins = np.arange(freqs, dtype=np.float64)[None, :]
    hann = 0.5 - 0.5 * np.cos(2.0 * math.pi * times / samples)
    angle = 2.0 * math.pi * bins * times / samples
    return np.concatenate([hann * np.cos(angle), -hann * np.sin(angle)], axis=1).astype(
        jnp.bfloat16
    )


def lag_tables(lags, freqs, samples):
    shift_lag = np.arange(lags, dtype=np.float64)[:, None] - lags // 2
    bins = np.arange(freqs, dtype=np.float64)[None, :]
    theta = 2.0 * math.pi * bins * shift_lag / samples
    cos = np.cos(theta).astype(jnp.bfloat16).astype(np.float32)
    sin = np.sin(theta).astype(jnp.bfloat16).astype(np.float32)
    return np.concatenate([cos, cos, -sin, sin], axis=1)


def in_vmem(value):
    return pltpu.with_memory_space_constraint(value, pltpu.VMEM)


VMEM_SPEC = pl.BlockSpec(memory_space=pltpu.VMEM)


def on_chip(kernel, name, out, *args):
    return pl.pallas_call(
        kernel,
        in_specs=[VMEM_SPEC] * len(args),
        out_specs=jax.tree.map(lambda _: VMEM_SPEC, out),
        out_shape=out,
        name=name,
    )(*[in_vmem(arg) for arg in args])


def whiten_kernel(raw_hbm, valid_hbm, basis_hbm, white_ref, raw_ref, valid_ref, basis_ref, sems):
    moves = ((raw_hbm, raw_ref), (basis_hbm, basis_ref), (valid_hbm, valid_ref))
    loads = [pltpu.make_async_copy(src, dst, sems.at[i]) for i, (src, dst) in enumerate(moves)]
    for load in loads:
        load.start()
    for load in loads:
        load.wait()
    chans, width = white_ref.shape[1:]
    spectra = jnp.dot(raw_ref[0], basis_ref[...], preferred_element_type=jnp.float32)
    power = jnp.mean(spectra * spectra, axis=-1, keepdims=True) + 1e-06
    mask = jnp.transpose(jnp.broadcast_to(valid_ref[...].astype(jnp.float32), (width, chans)))
    white_ref[0] = (spectra * lax.rsqrt(power) * mask).astype(jnp.bfloat16)


def whiten(raw, valid, basis):
    anywhere = pl.BlockSpec(memory_space=pl.ANY)
    return pl.pallas_call(
        whiten_kernel,
        in_specs=[anywhere] * 3,
        out_specs=VMEM_SPEC,
        out_shape=pltpu.VMEM(raw.shape, jnp.bfloat16),
        scratch_shapes=[
            pltpu.VMEM(raw.shape, raw.dtype),
            pltpu.VMEM(valid.shape, valid.dtype),
            pltpu.VMEM(basis.shape, basis.dtype),
            pltpu.SemaphoreType.DMA((3,)),
        ],
        name="whiten",
    )(raw, valid, basis)


def slots_of(chans):
    odd = lax.axis_index("pair") & 1
    return pl.multiple_of(odd * chans, chans), pl.multiple_of((1 - odd) * chans, chans)


def slots_kernel(white_ref, far_ref, send_ref):
    peers, both, _ = send_ref.shape
    chans = both // 2
    own_at, far_at = slots_of(chans)
    for peer in range(peers):
        send_ref[peer, pl.ds(own_at, chans), :] = white_ref[0]
        send_ref[peer, pl.ds(far_at, chans), :] = far_ref[0]


def far_kernel(gath_ref, table_ref, out_ref, mod_ref, *, scale):
    windows, both, width = gath_ref.shape
    chans = both // 2
    lag = pl.program_id(0)
    own_at, far_at = slots_of(chans)
    rows = pl.multiple_of(lag * chans, chans)
    turn = table_ref[pl.ds(lax.axis_index("tm") * pl.num_programs(0) + lag, 1), :]
    cos, sin = turn[:, :width], turn[:, width:]
    for w in range(windows):
        own = gath_ref[w, pl.ds(own_at, chans), :].astype(jnp.float32)
        turned = own * cos + pltpu.roll(own, width // 2, 1) * sin
        mod_ref[pl.ds(rows, chans), w * width : (w + 1) * width] = turned.astype(jnp.bfloat16)
    other = jnp.concatenate(
        [gath_ref[w, pl.ds(far_at, chans), :] for w in range(windows)], axis=1
    )
    total = lax.dot_general(
        mod_ref[pl.ds(rows, chans), :],
        other,
        (((1,), (1,)), ((), ())),
        preferred_element_type=jnp.float32,
    )
    out_ref[...] = total * scale


def correlate_far(gathered, table, lags, scale):
    windows, both, width = gathered.shape
    chans = both // 2
    return pl.pallas_call(
        functools.partial(far_kernel, scale=scale),
        grid=(lags,),
        in_specs=[VMEM_SPEC, VMEM_SPEC],
        out_specs=[pl.BlockSpec((chans, chans), lambda lag: (0, lag)), VMEM_SPEC],
        out_shape=[
            jax.ShapeDtypeStruct((chans, lags * chans), jnp.float32),
            pltpu.VMEM((lags * chans, windows * width), jnp.bfloat16),
        ],
        name="far_corr",
    )(in_vmem(gathered), in_vmem(table))


def corr_kernel(mod_ref, other_ref, out_ref, *, scale):
    windows, chans, _ = other_ref.shape
    rows = pl.multiple_of(pl.program_id(0) * chans, chans)
    other = jnp.concatenate([other_ref[w] for w in range(windows)], axis=1)
    total = lax.dot_general(
        mod_ref[pl.ds(rows, chans), :],
        other,
        (((1,), (1,)), ((), ())),
        preferred_element_type=jnp.float32,
    )
    out_ref[...] = total * scale


def correlate(mod, other, lags, scale, name):
    chans = other.shape[1]
    return pl.pallas_call(
        functools.partial(corr_kernel, scale=scale),
        grid=(lags,),
        in_specs=[VMEM_SPEC, VMEM_SPEC],
        out_specs=pl.BlockSpec((chans, chans), lambda lag: (0, lag)),
        out_shape=jax.ShapeDtypeStruct((chans, lags * chans), jnp.float32),
        name=name,
    )(in_vmem(mod), in_vmem(other))


def local(raw, valid):
    windows, chans, samples = raw.shape
    freqs = samples // 2
    groups = lax.axis_size("tm")
    pairs = lax.axis_size("pair")
    total = windows * groups
    lags = LAGS // groups
    scale = 1.0 / math.sqrt(total * freqs)
    basis = jnp.asarray(make_basis(samples, freqs))
    table = jnp.asarray(lag_tables(LAGS, freqs, samples))
    white = whiten(raw, valid, basis)
    far = lax.ppermute(white, "pair", [(p, (p - 2) % pairs) for p in range(pairs)])
    sends = on_chip(
        slots_kernel, "slots", pltpu.VMEM((total, 2 * chans, samples), jnp.bfloat16), white, far
    )
    gathered = lax.all_to_all(sends, "tm", 0, 0, tiled=True)
    near = lax.ppermute(gathered[:, chans:, :], "pair", [(p, p ^ 1) for p in range(pairs)])
    far_corr, mod = correlate_far(gathered, table, lags, scale)
    near_corr = correlate(mod, near, lags, scale, "near_corr")
    return (near_corr, far_corr)


def solution(mesh):
    return jax.shard_map(
        local,
        mesh=mesh,
        in_specs=(P("tm", "pair", None), P("tm", "pair")),
        out_specs=(P("pair", "tm"), P("pair", "tm")),
        check_vma=False,
    )
```

```python
import functools
import math

import jax
import jax.numpy as jnp
import numpy as np
from jax import lax
from jax.experimental import pallas as pl
from jax.experimental.pallas import tpu as pltpu
from jax.sharding import PartitionSpec as P

LAGS = 16


def make_basis(samples, freqs):
    times = np.arange(samples, dtype=np.float64)[:, None]
    bins = np.arange(freqs, dtype=np.float64)[None, :]
    hann = 0.5 - 0.5 * np.cos(2.0 * math.pi * times / samples)
    angle = 2.0 * math.pi * bins * times / samples
    return np.concatenate([hann * np.cos(angle), -hann * np.sin(angle)], axis=1).astype(
        jnp.bfloat16
    )


def lag_tables(lags, freqs, samples):
    shift_lag = np.arange(lags, dtype=np.float64)[:, None] - lags // 2
    bins = np.arange(freqs, dtype=np.float64)[None, :]
    theta = 2.0 * math.pi * bins * shift_lag / samples
    cos = np.cos(theta).astype(jnp.bfloat16).astype(np.float32)
    sin = np.sin(theta).astype(jnp.bfloat16).astype(np.float32)
    return np.concatenate([cos, cos, -sin, sin], axis=1)


def in_vmem(value):
    return pltpu.with_memory_space_constraint(value, pltpu.VMEM)


VMEM_SPEC = pl.BlockSpec(memory_space=pltpu.VMEM)


def on_chip(kernel, name, out, *args):
    return pl.pallas_call(
        kernel,
        in_specs=[VMEM_SPEC] * len(args),
        out_specs=jax.tree.map(lambda _: VMEM_SPEC, out),
        out_shape=out,
        name=name,
    )(*[in_vmem(arg) for arg in args])


def whiten_kernel(raw_hbm, valid_hbm, basis_hbm, *refs):
    *white_refs, raw_ref, valid_ref, basis_ref, sems = refs
    moves = ((raw_hbm, raw_ref), (basis_hbm, basis_ref), (valid_hbm, valid_ref))
    loads = [pltpu.make_async_copy(src, dst, sems.at[i]) for i, (src, dst) in enumerate(moves)]
    for load in loads:
        load.start()
    for load in loads:
        load.wait()
    chans, width = white_refs[0].shape[1:]
    spectra = jnp.dot(raw_ref[0], basis_ref[...], preferred_element_type=jnp.float32)
    power = jnp.mean(spectra * spectra, axis=-1, keepdims=True) + 1e-06
    mask = jnp.transpose(jnp.broadcast_to(valid_ref[...].astype(jnp.float32), (width, chans)))
    white = (spectra * lax.rsqrt(power) * mask).astype(jnp.bfloat16)
    for white_ref in white_refs:
        white_ref[0] = white


def whiten(raw, valid, basis, copies):
    anywhere = pl.BlockSpec(memory_space=pl.ANY)
    return pl.pallas_call(
        whiten_kernel,
        in_specs=[anywhere] * 3,
        out_specs=[VMEM_SPEC] * copies,
        out_shape=[pltpu.VMEM(raw.shape, jnp.bfloat16)] * copies,
        scratch_shapes=[
            pltpu.VMEM(raw.shape, raw.dtype),
            pltpu.VMEM(valid.shape, valid.dtype),
            pltpu.VMEM(basis.shape, basis.dtype),
            pltpu.SemaphoreType.DMA((3,)),
        ],
        name="whiten",
    )(raw, valid, basis)


def slots_of(chans):
    odd = lax.axis_index("pair") & 1
    return pl.multiple_of(odd * chans, chans), pl.multiple_of((1 - odd) * chans, chans)


def slots_kernel(white_ref, far_ref, send_ref):
    peers, both, _ = send_ref.shape
    chans = both // 2
    own_at, far_at = slots_of(chans)
    for peer in range(peers):
        send_ref[peer, pl.ds(own_at, chans), :] = white_ref[0]
        send_ref[peer, pl.ds(far_at, chans), :] = far_ref[0]


def spread_kernel(block_ref, send_ref):
    for peer in range(send_ref.shape[0]):
        send_ref[peer] = block_ref[0]


def merge_kernel(far_ref, early_ref, gath_ref):
    chans = far_ref.shape[1]
    own_at, far_at = slots_of(chans)
    for w in range(far_ref.shape[0]):
        gath_ref[w, pl.ds(own_at, chans), :] = early_ref[w]
        gath_ref[w, pl.ds(far_at, chans), :] = far_ref[w]


def place_kernel(own_ref, gath_ref):
    chans = own_ref.shape[1]
    own_at, _ = slots_of(chans)
    for w in range(own_ref.shape[0]):
        gath_ref[w, pl.ds(own_at, chans), :] = own_ref[w]


def put_far_kernel(far_ref, old_ref, gath_ref):
    del old_ref
    chans = far_ref.shape[1]
    _, far_at = slots_of(chans)
    for w in range(far_ref.shape[0]):
        gath_ref[w, pl.ds(far_at, chans), :] = far_ref[w]


def unwritten(shape, dtype):
    return pl.pallas_call(
        lambda out_ref: None,
        out_specs=pl.BlockSpec(memory_space=pl.ANY),
        out_shape=jax.ShapeDtypeStruct(shape, dtype),
        name="unwritten",
    )()


def far_kernel(gath_ref, table_ref, out_ref, mod_ref, *, scale):
    windows, both, width = gath_ref.shape
    chans = both // 2
    lag = pl.program_id(0)
    own_at, far_at = slots_of(chans)
    rows = pl.multiple_of(lag * chans, chans)
    turn = table_ref[pl.ds(lax.axis_index("tm") * pl.num_programs(0) + lag, 1), :]
    cos, sin = turn[:, :width], turn[:, width:]
    for w in range(windows):
        own = gath_ref[w, pl.ds(own_at, chans), :].astype(jnp.float32)
        turned = own * cos + pltpu.roll(own, width // 2, 1) * sin
        mod_ref[pl.ds(rows, chans), w * width : (w + 1) * width] = turned.astype(jnp.bfloat16)
    other = jnp.concatenate(
        [gath_ref[w, pl.ds(far_at, chans), :] for w in range(windows)], axis=1
    )
    total = lax.dot_general(
        mod_ref[pl.ds(rows, chans), :],
        other,
        (((1,), (1,)), ((), ())),
        preferred_element_type=jnp.float32,
    )
    out_ref[...] = total * scale


def correlate_far(gathered, table, lags, scale):
    windows, both, width = gathered.shape
    chans = both // 2
    return pl.pallas_call(
        functools.partial(far_kernel, scale=scale),
        grid=(lags,),
        in_specs=[VMEM_SPEC, VMEM_SPEC],
        out_specs=[pl.BlockSpec((chans, chans), lambda lag: (0, lag)), VMEM_SPEC],
        out_shape=[
            jax.ShapeDtypeStruct((chans, lags * chans), jnp.float32),
            pltpu.VMEM((lags * chans, windows * width), jnp.bfloat16),
        ],
        name="far_corr",
    )(in_vmem(gathered), in_vmem(table))


def corr_kernel(mod_ref, other_ref, out_ref, *, scale):
    windows, chans, _ = other_ref.shape
    rows = pl.multiple_of(pl.program_id(0) * chans, chans)
    other = jnp.concatenate([other_ref[w] for w in range(windows)], axis=1)
    total = lax.dot_general(
        mod_ref[pl.ds(rows, chans), :],
        other,
        (((1,), (1,)), ((), ())),
        preferred_element_type=jnp.float32,
    )
    out_ref[...] = total * scale


def correlate(mod, other, lags, scale, name):
    chans = other.shape[1]
    return pl.pallas_call(
        functools.partial(corr_kernel, scale=scale),
        grid=(lags,),
        in_specs=[VMEM_SPEC, VMEM_SPEC],
        out_specs=pl.BlockSpec((chans, chans), lambda lag: (0, lag)),
        out_shape=jax.ShapeDtypeStruct((chans, lags * chans), jnp.float32),
        name=name,
    )(in_vmem(mod), in_vmem(other))


def gather_windows(whites, pairs, groups):
    white, for_start, for_both, for_end = whites
    windows, chans, width = white.shape
    total = windows * groups
    at_start = lax.axis_index("pair") < 2
    at_end = lax.axis_index("pair") >= pairs - 2
    single = pltpu.VMEM((total, chans, width), white.dtype)
    double = pltpu.VMEM((total, 2 * chans, width), white.dtype)

    def exchange(sends):
        return lax.all_to_all(sends, "tm", 0, 0, tiled=True)

    def one(block):
        return exchange(on_chip(spread_kernel, "spread", single, block))

    def both(white, far):
        return exchange(on_chip(slots_kernel, "slots", double, white, far))

    def after_own(far, own):
        return on_chip(merge_kernel, "merge", double, one(far), own)

    def own_alone(white):
        return on_chip(place_kernel, "place_own", double, one(white))

    def add_far(wrapped, gathered):
        return pl.pallas_call(
            put_far_kernel,
            in_specs=[VMEM_SPEC] * 2,
            out_specs=VMEM_SPEC,
            out_shape=double,
            input_output_aliases={1: 0},
            name="put_far",
        )(in_vmem(one(wrapped)), in_vmem(gathered))

    far = lax.ppermute(white, "pair", [(p, p - 2) for p in range(2, pairs)])
    own = lax.cond(at_start, one, lambda white: unwritten(single.shape, single.dtype), for_start)
    white, own = lax.optimization_barrier((white, own))
    wrapped = lax.ppermute(white, "pair", [(0, pairs - 2), (1, pairs - 1)])
    gathered = lax.switch(
        at_start.astype(jnp.int32) + 2 * at_end.astype(jnp.int32),
        (
            lambda for_both, for_end, far, own: both(for_both, far),
            lambda for_both, for_end, far, own: after_own(far, own),
            lambda for_both, for_end, far, own: own_alone(for_end),
        ),
        for_both,
        for_end,
        far,
        own,
    )
    return lax.cond(at_end, add_far, lambda wrapped, gathered: gathered, wrapped, gathered)


def local(raw, valid):
    windows, chans, samples = raw.shape
    freqs = samples // 2
    groups = lax.axis_size("tm")
    pairs = lax.axis_size("pair")
    total = windows * groups
    lags = LAGS // groups
    scale = 1.0 / math.sqrt(total * freqs)
    basis = jnp.asarray(make_basis(samples, freqs))
    table = jnp.asarray(lag_tables(LAGS, freqs, samples))
    whites = whiten(raw, valid, basis, 4)
    gathered = gather_windows(whites, pairs, groups)
    near = lax.ppermute(gathered[:, chans:, :], "pair", [(p, p ^ 1) for p in range(pairs)])
    far_corr, mod = correlate_far(gathered, table, lags, scale)
    near_corr = correlate(mod, near, lags, scale, "near_corr")
    return (near_corr, far_corr)


def solution(mesh):
    return jax.shard_map(
        local,
        mesh=mesh,
        in_specs=(P("tm", "pair", None), P("tm", "pair")),
        out_specs=(P("pair", "tm"), P("pair", "tm")),
        check_vma=False,
    )
```

```python
import functools
import math

import jax
import jax.numpy as jnp
import numpy as np
from jax import lax
from jax.experimental import pallas as pl
from jax.experimental.pallas import tpu as pltpu
from jax.sharding import PartitionSpec as P

LAGS = 16


def make_basis(samples, freqs):
    times = np.arange(samples, dtype=np.float64)[:, None]
    bins = np.arange(freqs, dtype=np.float64)[None, :]
    hann = 0.5 - 0.5 * np.cos(2.0 * math.pi * times / samples)
    angle = 2.0 * math.pi * bins * times / samples
    return np.concatenate([hann * np.cos(angle), -hann * np.sin(angle)], axis=1).astype(
        jnp.bfloat16
    )


def lag_tables(lags, freqs, samples):
    shift_lag = np.arange(lags, dtype=np.float64)[:, None] - lags // 2
    bins = np.arange(freqs, dtype=np.float64)[None, :]
    theta = 2.0 * math.pi * bins * shift_lag / samples
    cos = np.cos(theta).astype(jnp.bfloat16).astype(np.float32)
    sin = np.sin(theta).astype(jnp.bfloat16).astype(np.float32)
    return np.concatenate([cos, cos, -sin, sin], axis=1)


def in_vmem(value):
    return pltpu.with_memory_space_constraint(value, pltpu.VMEM)


VMEM_SPEC = pl.BlockSpec(memory_space=pltpu.VMEM)


def on_chip(kernel, name, out, *args):
    return pl.pallas_call(
        kernel,
        in_specs=[VMEM_SPEC] * len(args),
        out_specs=jax.tree.map(lambda _: VMEM_SPEC, out),
        out_shape=out,
        name=name,
    )(*[in_vmem(arg) for arg in args])


def whiten_kernel(raw_hbm, valid_hbm, basis_hbm, *refs):
    *white_refs, raw_ref, valid_ref, basis_ref, sems = refs
    moves = ((raw_hbm, raw_ref), (basis_hbm, basis_ref), (valid_hbm, valid_ref))
    loads = [pltpu.make_async_copy(src, dst, sems.at[i]) for i, (src, dst) in enumerate(moves)]
    for load in loads:
        load.start()
    for load in loads:
        load.wait()
    chans, width = white_refs[0].shape[1:]
    spectra = jnp.dot(raw_ref[0], basis_ref[...], preferred_element_type=jnp.float32)
    power = jnp.mean(spectra * spectra, axis=-1, keepdims=True) + 1e-06
    mask = jnp.transpose(jnp.broadcast_to(valid_ref[...].astype(jnp.float32), (width, chans)))
    white = (spectra * lax.rsqrt(power) * mask).astype(jnp.bfloat16)
    for white_ref in white_refs:
        white_ref[0] = white


def whiten(raw, valid, basis, copies):
    anywhere = pl.BlockSpec(memory_space=pl.ANY)
    return pl.pallas_call(
        whiten_kernel,
        in_specs=[anywhere] * 3,
        out_specs=[VMEM_SPEC] * copies,
        out_shape=[pltpu.VMEM(raw.shape, jnp.bfloat16)] * copies,
        scratch_shapes=[
            pltpu.VMEM(raw.shape, raw.dtype),
            pltpu.VMEM(valid.shape, valid.dtype),
            pltpu.VMEM(basis.shape, basis.dtype),
            pltpu.SemaphoreType.DMA((3,)),
        ],
        name="whiten",
    )(raw, valid, basis)


def slots_of(chans):
    odd = lax.axis_index("pair") & 1
    return pl.multiple_of(odd * chans, chans), pl.multiple_of((1 - odd) * chans, chans)


def slots_kernel(white_ref, far_ref, send_ref):
    peers, both, _ = send_ref.shape
    chans = both // 2
    own_at, far_at = slots_of(chans)
    for peer in range(peers):
        send_ref[peer, pl.ds(own_at, chans), :] = white_ref[0]
        send_ref[peer, pl.ds(far_at, chans), :] = far_ref[0]


def spread_kernel(block_ref, send_ref):
    for peer in range(send_ref.shape[0]):
        send_ref[peer] = block_ref[0]


def merge_kernel(far_ref, early_ref, gath_ref):
    chans = far_ref.shape[1]
    own_at, far_at = slots_of(chans)
    for w in range(far_ref.shape[0]):
        gath_ref[w, pl.ds(own_at, chans), :] = early_ref[w]
        gath_ref[w, pl.ds(far_at, chans), :] = far_ref[w]


def place_kernel(own_ref, gath_ref):
    chans = own_ref.shape[1]
    own_at, _ = slots_of(chans)
    for w in range(own_ref.shape[0]):
        gath_ref[w, pl.ds(own_at, chans), :] = own_ref[w]


def put_far_kernel(far_ref, old_ref, gath_ref):
    del old_ref
    chans = far_ref.shape[1]
    _, far_at = slots_of(chans)
    for w in range(far_ref.shape[0]):
        gath_ref[w, pl.ds(far_at, chans), :] = far_ref[w]


def unwritten(shape, dtype):
    return pl.pallas_call(
        lambda out_ref: None,
        out_specs=pl.BlockSpec(memory_space=pl.ANY),
        out_shape=jax.ShapeDtypeStruct(shape, dtype),
        name="unwritten",
    )()


def far_kernel(gath_ref, table_ref, out_ref, mod_ref, *, scale):
    windows, both, width = gath_ref.shape
    chans = both // 2
    lag = pl.program_id(0)
    own_at, far_at = slots_of(chans)
    rows = pl.multiple_of(lag * chans, chans)
    turn = table_ref[pl.ds(lax.axis_index("tm") * pl.num_programs(0) + lag, 1), :]
    cos, sin = turn[:, :width], turn[:, width:]
    for w in range(windows):
        own = gath_ref[w, pl.ds(own_at, chans), :].astype(jnp.float32)
        turned = own * cos + pltpu.roll(own, width // 2, 1) * sin
        mod_ref[pl.ds(rows, chans), w * width : (w + 1) * width] = turned.astype(jnp.bfloat16)
    other = jnp.concatenate(
        [gath_ref[w, pl.ds(far_at, chans), :] for w in range(windows)], axis=1
    )
    total = lax.dot_general(
        mod_ref[pl.ds(rows, chans), :],
        other,
        (((1,), (1,)), ((), ())),
        preferred_element_type=jnp.float32,
    )
    out_ref[...] = total * scale


def correlate_far(gathered, table, lags, scale):
    windows, both, width = gathered.shape
    chans = both // 2
    return pl.pallas_call(
        functools.partial(far_kernel, scale=scale),
        grid=(lags,),
        in_specs=[VMEM_SPEC, VMEM_SPEC],
        out_specs=[pl.BlockSpec((chans, chans), lambda lag: (0, lag)), VMEM_SPEC],
        out_shape=[
            jax.ShapeDtypeStruct((chans, lags * chans), jnp.float32),
            pltpu.VMEM((lags * chans, windows * width), jnp.bfloat16),
        ],
        name="far_corr",
    )(in_vmem(gathered), in_vmem(table))


def corr_kernel(mod_ref, other_ref, out_ref, *, scale):
    windows, chans, _ = other_ref.shape
    other = jnp.concatenate([other_ref[w] for w in range(windows)], axis=1)
    total = lax.dot_general(
        mod_ref[...], other, (((1,), (1,)), ((), ())), preferred_element_type=jnp.float32
    )
    for lag in range(total.shape[0] // chans):
        rows = slice(lag * chans, (lag + 1) * chans)
        out_ref[:, rows] = total[rows] * scale


def correlate(mod, other, lags, scale, name):
    chans = other.shape[1]
    return pl.pallas_call(
        functools.partial(corr_kernel, scale=scale),
        in_specs=[VMEM_SPEC, VMEM_SPEC],
        out_specs=VMEM_SPEC,
        out_shape=jax.ShapeDtypeStruct((chans, lags * chans), jnp.float32),
        name=name,
    )(in_vmem(mod), in_vmem(other))


def gather_windows(whites, pairs, groups):
    white, for_start, for_both, for_end = whites
    windows, chans, width = white.shape
    total = windows * groups
    at_start = lax.axis_index("pair") < 2
    at_end = lax.axis_index("pair") >= pairs - 2
    single = pltpu.VMEM((total, chans, width), white.dtype)
    double = pltpu.VMEM((total, 2 * chans, width), white.dtype)

    def exchange(sends):
        return lax.all_to_all(sends, "tm", 0, 0, tiled=True)

    def one(block):
        return exchange(on_chip(spread_kernel, "spread", single, block))

    def both(white, far):
        return exchange(on_chip(slots_kernel, "slots", double, white, far))

    def after_own(far, own):
        return on_chip(merge_kernel, "merge", double, one(far), own)

    def add_far(wrapped, gathered):
        return pl.pallas_call(
            put_far_kernel,
            in_specs=[VMEM_SPEC] * 2,
            out_specs=VMEM_SPEC,
            out_shape=double,
            input_output_aliases={1: 0},
            name="put_far",
        )(in_vmem(one(wrapped)), in_vmem(gathered))

    far = lax.ppermute(white, "pair", [(p, p - 2) for p in range(2, pairs)])
    own = lax.cond(at_start, one, lambda white: unwritten(single.shape, single.dtype), for_start)
    white, own = lax.optimization_barrier((white, own))
    wrapped = lax.ppermute(white, "pair", [(0, pairs - 2), (1, pairs - 1)])
    own = lax.cond(at_end, lambda block, own: one(block), lambda block, own: own, for_end, own)
    gathered = lax.switch(
        at_start.astype(jnp.int32) + 2 * at_end.astype(jnp.int32),
        (
            lambda for_both, far, own: both(for_both, far),
            lambda for_both, far, own: after_own(far, own),
            lambda for_both, far, own: on_chip(place_kernel, "place_own", double, own),
        ),
        for_both,
        far,
        own,
    )
    return lax.cond(at_end, add_far, lambda wrapped, gathered: gathered, wrapped, gathered)


def local(raw, valid):
    windows, chans, samples = raw.shape
    freqs = samples // 2
    groups = lax.axis_size("tm")
    pairs = lax.axis_size("pair")
    total = windows * groups
    lags = LAGS // groups
    scale = 1.0 / math.sqrt(total * freqs)
    basis = jnp.asarray(make_basis(samples, freqs))
    table = jnp.asarray(lag_tables(LAGS, freqs, samples))
    whites = whiten(raw, valid, basis, 4)
    gathered = gather_windows(whites, pairs, groups)
    near = lax.ppermute(gathered[:, chans:, :], "pair", [(p, p ^ 1) for p in range(pairs)])
    far_corr, mod = correlate_far(gathered, table, lags, scale)
    near_corr = correlate(mod, near, lags, scale, "near_corr")
    return (near_corr, far_corr)


def solution(mesh):
    return jax.shard_map(
        local,
        mesh=mesh,
        in_specs=(P("tm", "pair", None), P("tm", "pair")),
        out_specs=(P("pair", "tm"), P("pair", "tm")),
        check_vma=False,
    )
```

```python
import functools
import math

import jax
import jax.numpy as jnp
import numpy as np
from jax import lax
from jax.experimental import pallas as pl
from jax.experimental.pallas import tpu as pltpu
from jax.sharding import PartitionSpec as P

LAGS = 16


def make_basis(samples, freqs):
    times = np.arange(samples, dtype=np.float64)[:, None]
    bins = np.arange(freqs, dtype=np.float64)[None, :]
    hann = 0.5 - 0.5 * np.cos(2.0 * math.pi * times / samples)
    angle = 2.0 * math.pi * bins * times / samples
    return np.concatenate([hann * np.cos(angle), -hann * np.sin(angle)], axis=1).astype(
        jnp.bfloat16
    )


def lag_tables(lags, freqs, samples):
    shift_lag = np.arange(lags, dtype=np.float64)[:, None] - lags // 2
    bins = np.arange(freqs, dtype=np.float64)[None, :]
    theta = 2.0 * math.pi * bins * shift_lag / samples
    cos = np.cos(theta).astype(jnp.bfloat16).astype(np.float32)
    sin = np.sin(theta).astype(jnp.bfloat16).astype(np.float32)
    return np.concatenate([cos, cos, -sin, sin], axis=1)


def in_vmem(value):
    return pltpu.with_memory_space_constraint(value, pltpu.VMEM)


VMEM_SPEC = pl.BlockSpec(memory_space=pltpu.VMEM)


def on_chip(kernel, name, out, *args):
    return pl.pallas_call(
        kernel,
        in_specs=[VMEM_SPEC] * len(args),
        out_specs=jax.tree.map(lambda _: VMEM_SPEC, out),
        out_shape=out,
        name=name,
    )(*[in_vmem(arg) for arg in args])


def whiten_kernel(raw_hbm, valid_hbm, basis_hbm, *refs):
    *white_refs, raw_ref, valid_ref, basis_ref, sems = refs
    moves = ((raw_hbm, raw_ref), (basis_hbm, basis_ref), (valid_hbm, valid_ref))
    loads = [pltpu.make_async_copy(src, dst, sems.at[i]) for i, (src, dst) in enumerate(moves)]
    for load in loads:
        load.start()
    for load in loads:
        load.wait()
    chans, width = white_refs[0].shape[1:]
    spectra = jnp.dot(raw_ref[0], basis_ref[...], preferred_element_type=jnp.float32)
    power = jnp.mean(spectra * spectra, axis=-1, keepdims=True) + 1e-06
    mask = jnp.transpose(jnp.broadcast_to(valid_ref[...].astype(jnp.float32), (width, chans)))
    white = (spectra * lax.rsqrt(power) * mask).astype(jnp.bfloat16)
    for white_ref in white_refs:
        white_ref[0] = white


def whiten(raw, valid, basis, copies):
    anywhere = pl.BlockSpec(memory_space=pl.ANY)
    return pl.pallas_call(
        whiten_kernel,
        in_specs=[anywhere] * 3,
        out_specs=[VMEM_SPEC] * copies,
        out_shape=[pltpu.VMEM(raw.shape, jnp.bfloat16)] * copies,
        scratch_shapes=[
            pltpu.VMEM(raw.shape, raw.dtype),
            pltpu.VMEM(valid.shape, valid.dtype),
            pltpu.VMEM(basis.shape, basis.dtype),
            pltpu.SemaphoreType.DMA((3,)),
        ],
        name="whiten",
    )(raw, valid, basis)


def slots_of(chans):
    odd = lax.axis_index("pair") & 1
    return pl.multiple_of(odd * chans, chans), pl.multiple_of((1 - odd) * chans, chans)


def slots_kernel(white_ref, far_ref, send_ref):
    peers, both, _ = send_ref.shape
    chans = both // 2
    own_at, far_at = slots_of(chans)
    for peer in range(peers):
        send_ref[peer, pl.ds(own_at, chans), :] = white_ref[0]
        send_ref[peer, pl.ds(far_at, chans), :] = far_ref[0]


def spread_kernel(block_ref, send_ref):
    for peer in range(send_ref.shape[0]):
        send_ref[peer] = block_ref[0]


def merge_kernel(far_ref, early_ref, gath_ref):
    chans = far_ref.shape[1]
    own_at, far_at = slots_of(chans)
    for w in range(far_ref.shape[0]):
        gath_ref[w, pl.ds(own_at, chans), :] = early_ref[w]
        gath_ref[w, pl.ds(far_at, chans), :] = far_ref[w]


def place_kernel(own_ref, gath_ref):
    chans = own_ref.shape[1]
    own_at, _ = slots_of(chans)
    for w in range(own_ref.shape[0]):
        gath_ref[w, pl.ds(own_at, chans), :] = own_ref[w]


def put_far_kernel(far_ref, old_ref, gath_ref):
    del old_ref
    chans = far_ref.shape[1]
    _, far_at = slots_of(chans)
    for w in range(far_ref.shape[0]):
        gath_ref[w, pl.ds(far_at, chans), :] = far_ref[w]


def unwritten(shape, dtype):
    return pl.pallas_call(
        lambda out_ref: None,
        out_specs=pl.BlockSpec(memory_space=pl.ANY),
        out_shape=jax.ShapeDtypeStruct(shape, dtype),
        name="unwritten",
    )()


def far_kernel(gath_ref, table_ref, out_hbm, mod_ref, out_ref, sems, *, scale):
    windows, both, width = gath_ref.shape
    chans = both // 2
    own_at, far_at = slots_of(chans)
    lags = mod_ref.shape[0] // chans
    other = jnp.concatenate(
        [gath_ref[w, pl.ds(far_at, chans), :] for w in range(windows)], axis=1
    )
    turns = [table_ref[pl.ds(lax.axis_index("tm") * lags + lag, 1), :] for lag in range(lags)]
    writes = []
    for lag, turn in enumerate(turns):
        rows = slice(lag * chans, (lag + 1) * chans)
        cos, sin = turn[:, :width], turn[:, width:]
        for w in range(windows):
            own = gath_ref[w, pl.ds(own_at, chans), :].astype(jnp.float32)
            turned = own * cos + pltpu.roll(own, width // 2, 1) * sin
            mod_ref[rows, w * width : (w + 1) * width] = turned.astype(jnp.bfloat16)
        total = lax.dot_general(
            mod_ref[rows, :], other, (((1,), (1,)), ((), ())), preferred_element_type=jnp.float32
        )
        out_ref[lag] = total * scale
        write = pltpu.make_async_copy(out_ref.at[lag], out_hbm.at[:, rows], sems.at[lag])
        write.start()
        writes.append(write)
    for write in writes:
        write.wait()


def correlate_far(gathered, table, lags, scale):
    windows, both, width = gathered.shape
    chans = both // 2
    return pl.pallas_call(
        functools.partial(far_kernel, scale=scale),
        in_specs=[VMEM_SPEC, VMEM_SPEC],
        out_specs=[pl.BlockSpec(memory_space=pl.ANY), VMEM_SPEC],
        out_shape=[
            jax.ShapeDtypeStruct((chans, lags * chans), jnp.float32),
            pltpu.VMEM((lags * chans, windows * width), jnp.bfloat16),
        ],
        scratch_shapes=[
            pltpu.VMEM((lags, chans, chans), jnp.float32),
            pltpu.SemaphoreType.DMA((lags,)),
        ],
        name="far_corr",
    )(in_vmem(gathered), in_vmem(table))


def corr_kernel(mod_ref, other_ref, out_ref, *, scale):
    windows, chans, _ = other_ref.shape
    other = jnp.concatenate([other_ref[w] for w in range(windows)], axis=1)
    total = lax.dot_general(
        mod_ref[...], other, (((1,), (1,)), ((), ())), preferred_element_type=jnp.float32
    )
    for lag in range(total.shape[0] // chans):
        rows = slice(lag * chans, (lag + 1) * chans)
        out_ref[:, rows] = total[rows] * scale


def correlate(mod, other, lags, scale, name):
    chans = other.shape[1]
    return pl.pallas_call(
        functools.partial(corr_kernel, scale=scale),
        in_specs=[VMEM_SPEC, VMEM_SPEC],
        out_specs=VMEM_SPEC,
        out_shape=jax.ShapeDtypeStruct((chans, lags * chans), jnp.float32),
        name=name,
    )(in_vmem(mod), in_vmem(other))


def gather_windows(whites, pairs, groups):
    white, for_start, for_both, for_end = whites
    windows, chans, width = white.shape
    total = windows * groups
    at_start = lax.axis_index("pair") < 2
    at_end = lax.axis_index("pair") >= pairs - 2
    single = pltpu.VMEM((total, chans, width), white.dtype)
    double = pltpu.VMEM((total, 2 * chans, width), white.dtype)

    def exchange(sends):
        return lax.all_to_all(sends, "tm", 0, 0, tiled=True)

    def one(block):
        return exchange(on_chip(spread_kernel, "spread", single, block))

    def both(white, far):
        return exchange(on_chip(slots_kernel, "slots", double, white, far))

    def after_own(far, own):
        return on_chip(merge_kernel, "merge", double, one(far), own)

    def add_far(wrapped, gathered):
        return pl.pallas_call(
            put_far_kernel,
            in_specs=[VMEM_SPEC] * 2,
            out_specs=VMEM_SPEC,
            out_shape=double,
            input_output_aliases={1: 0},
            name="put_far",
        )(in_vmem(one(wrapped)), in_vmem(gathered))

    far = lax.ppermute(white, "pair", [(p, p - 2) for p in range(2, pairs)])
    own = lax.cond(at_start, one, lambda white: unwritten(single.shape, single.dtype), for_start)
    white, own = lax.optimization_barrier((white, own))
    wrapped = lax.ppermute(white, "pair", [(0, pairs - 2), (1, pairs - 1)])
    own = lax.cond(at_end, lambda block, own: one(block), lambda block, own: own, for_end, own)
    gathered = lax.switch(
        at_start.astype(jnp.int32) + 2 * at_end.astype(jnp.int32),
        (
            lambda for_both, far, own: both(for_both, far),
            lambda for_both, far, own: after_own(far, own),
            lambda for_both, far, own: on_chip(place_kernel, "place_own", double, own),
        ),
        for_both,
        far,
        own,
    )
    return lax.cond(at_end, add_far, lambda wrapped, gathered: gathered, wrapped, gathered)


def local(raw, valid):
    windows, chans, samples = raw.shape
    freqs = samples // 2
    groups = lax.axis_size("tm")
    pairs = lax.axis_size("pair")
    total = windows * groups
    lags = LAGS // groups
    scale = 1.0 / math.sqrt(total * freqs)
    basis = jnp.asarray(make_basis(samples, freqs))
    table = jnp.asarray(lag_tables(LAGS, freqs, samples))
    whites = whiten(raw, valid, basis, 4)
    gathered = gather_windows(whites, pairs, groups)
    near = lax.ppermute(gathered[:, chans:, :], "pair", [(p, p ^ 1) for p in range(pairs)])
    far_corr, mod = correlate_far(gathered, table, lags, scale)
    near_corr = correlate(mod, near, lags, scale, "near_corr")
    return (near_corr, far_corr)


def solution(mesh):
    return jax.shard_map(
        local,
        mesh=mesh,
        in_specs=(P("tm", "pair", None), P("tm", "pair")),
        out_specs=(P("pair", "tm"), P("pair", "tm")),
        check_vma=False,
    )
```

```python
import functools
import math

import jax
import jax.numpy as jnp
import numpy as np
from jax import lax
from jax.experimental import pallas as pl
from jax.experimental.pallas import tpu as pltpu
from jax.sharding import PartitionSpec as P

LAGS = 16


def make_basis(samples, freqs):
    times = np.arange(samples, dtype=np.float64)[:, None]
    bins = np.arange(freqs, dtype=np.float64)[None, :]
    hann = 0.5 - 0.5 * np.cos(2.0 * math.pi * times / samples)
    angle = 2.0 * math.pi * bins * times / samples
    return np.concatenate([hann * np.cos(angle), -hann * np.sin(angle)], axis=1).astype(
        jnp.bfloat16
    )


def lag_tables(lags, freqs, samples):
    shift_lag = np.arange(lags, dtype=np.float64)[:, None] - lags // 2
    bins = np.arange(freqs, dtype=np.float64)[None, :]
    theta = 2.0 * math.pi * bins * shift_lag / samples
    cos = np.cos(theta).astype(jnp.bfloat16).astype(np.float32)
    sin = np.sin(theta).astype(jnp.bfloat16).astype(np.float32)
    return np.concatenate([cos, cos, -sin, sin], axis=1)


def in_vmem(value):
    return pltpu.with_memory_space_constraint(value, pltpu.VMEM)


VMEM_SPEC = pl.BlockSpec(memory_space=pltpu.VMEM)


def on_chip(kernel, name, out, *args):
    return pl.pallas_call(
        kernel,
        in_specs=[VMEM_SPEC] * len(args),
        out_specs=jax.tree.map(lambda _: VMEM_SPEC, out),
        out_shape=out,
        name=name,
    )(*[in_vmem(arg) for arg in args])


def whiten_kernel(raw_hbm, valid_hbm, basis_hbm, *refs):
    *white_refs, raw_ref, valid_ref, basis_ref, sems = refs
    moves = ((raw_hbm, raw_ref), (basis_hbm, basis_ref), (valid_hbm, valid_ref))
    loads = [pltpu.make_async_copy(src, dst, sems.at[i]) for i, (src, dst) in enumerate(moves)]
    for load in loads:
        load.start()
    for load in loads:
        load.wait()
    chans, width = white_refs[0].shape[1:]
    spectra = jnp.dot(raw_ref[0], basis_ref[...], preferred_element_type=jnp.float32)
    power = jnp.mean(spectra * spectra, axis=-1, keepdims=True) + 1e-06
    mask = jnp.transpose(jnp.broadcast_to(valid_ref[...].astype(jnp.float32), (width, chans)))
    white = (spectra * lax.rsqrt(power) * mask).astype(jnp.bfloat16)
    for white_ref in white_refs:
        white_ref[0] = white


def whiten(raw, valid, basis, copies):
    anywhere = pl.BlockSpec(memory_space=pl.ANY)
    return pl.pallas_call(
        whiten_kernel,
        in_specs=[anywhere] * 3,
        out_specs=[VMEM_SPEC] * copies,
        out_shape=[pltpu.VMEM(raw.shape, jnp.bfloat16)] * copies,
        scratch_shapes=[
            pltpu.VMEM(raw.shape, raw.dtype),
            pltpu.VMEM(valid.shape, valid.dtype),
            pltpu.VMEM(basis.shape, basis.dtype),
            pltpu.SemaphoreType.DMA((3,)),
        ],
        name="whiten",
    )(raw, valid, basis)


def slots_of(chans):
    odd = lax.axis_index("pair") & 1
    return pl.multiple_of(odd * chans, chans), pl.multiple_of((1 - odd) * chans, chans)


def slots_kernel(white_ref, far_ref, send_ref):
    peers, both, _ = send_ref.shape
    chans = both // 2
    own_at, far_at = slots_of(chans)
    for peer in range(peers):
        send_ref[peer, pl.ds(own_at, chans), :] = white_ref[0]
        send_ref[peer, pl.ds(far_at, chans), :] = far_ref[0]


def spread_kernel(block_ref, send_ref):
    for peer in range(send_ref.shape[0]):
        send_ref[peer] = block_ref[0]


def merge_kernel(far_ref, early_ref, gath_ref):
    chans = far_ref.shape[1]
    own_at, far_at = slots_of(chans)
    for w in range(far_ref.shape[0]):
        gath_ref[w, pl.ds(own_at, chans), :] = early_ref[w]
        gath_ref[w, pl.ds(far_at, chans), :] = far_ref[w]


def place_kernel(own_ref, gath_ref):
    chans = own_ref.shape[1]
    own_at, _ = slots_of(chans)
    for w in range(own_ref.shape[0]):
        gath_ref[w, pl.ds(own_at, chans), :] = own_ref[w]


def put_far_kernel(far_ref, old_ref, gath_ref):
    del old_ref
    chans = far_ref.shape[1]
    _, far_at = slots_of(chans)
    for w in range(far_ref.shape[0]):
        gath_ref[w, pl.ds(far_at, chans), :] = far_ref[w]


def put_both_kernel(block_ref, old_ref, out_ref):
    del old_ref
    out_ref[...] = block_ref[...]


def unwritten(shape, dtype):
    return pl.pallas_call(
        lambda out_ref: None,
        out_specs=pl.BlockSpec(memory_space=pl.ANY),
        out_shape=jax.ShapeDtypeStruct(shape, dtype),
        name="unwritten",
    )()


def far_kernel(gath_ref, table_ref, out_hbm, mod_ref, out_ref, sems, *, scale):
    windows, both, width = gath_ref.shape
    chans = both // 2
    own_at, far_at = slots_of(chans)
    lags = mod_ref.shape[0] // chans
    other = jnp.concatenate(
        [gath_ref[w, pl.ds(far_at, chans), :] for w in range(windows)], axis=1
    )
    turns = [table_ref[pl.ds(lax.axis_index("tm") * lags + lag, 1), :] for lag in range(lags)]
    writes = []
    for lag, turn in enumerate(turns):
        rows = slice(lag * chans, (lag + 1) * chans)
        cos, sin = turn[:, :width], turn[:, width:]
        for w in range(windows):
            own = gath_ref[w, pl.ds(own_at, chans), :].astype(jnp.float32)
            turned = own * cos + pltpu.roll(own, width // 2, 1) * sin
            mod_ref[rows, w * width : (w + 1) * width] = turned.astype(jnp.bfloat16)
        total = lax.dot_general(
            mod_ref[rows, :], other, (((1,), (1,)), ((), ())), preferred_element_type=jnp.float32
        )
        out_ref[lag] = total * scale
        write = pltpu.make_async_copy(out_ref.at[lag], out_hbm.at[:, rows], sems.at[lag])
        write.start()
        writes.append(write)
    for write in writes:
        write.wait()


def correlate_far(gathered, table, lags, scale):
    windows, both, width = gathered.shape
    chans = both // 2
    return pl.pallas_call(
        functools.partial(far_kernel, scale=scale),
        in_specs=[VMEM_SPEC, VMEM_SPEC],
        out_specs=[pl.BlockSpec(memory_space=pl.ANY), VMEM_SPEC],
        out_shape=[
            jax.ShapeDtypeStruct((chans, lags * chans), jnp.float32),
            pltpu.VMEM((lags * chans, windows * width), jnp.bfloat16),
        ],
        scratch_shapes=[
            pltpu.VMEM((lags, chans, chans), jnp.float32),
            pltpu.SemaphoreType.DMA((lags,)),
        ],
        name="far_corr",
    )(in_vmem(gathered), in_vmem(table))


def corr_kernel(mod_ref, other_ref, out_ref, *, scale):
    windows, chans, _ = other_ref.shape
    other = jnp.concatenate([other_ref[w] for w in range(windows)], axis=1)
    total = lax.dot_general(
        mod_ref[...], other, (((1,), (1,)), ((), ())), preferred_element_type=jnp.float32
    )
    for lag in range(total.shape[0] // chans):
        rows = slice(lag * chans, (lag + 1) * chans)
        out_ref[:, rows] = total[rows] * scale


def correlate(mod, other, lags, scale, name):
    chans = other.shape[1]
    return pl.pallas_call(
        functools.partial(corr_kernel, scale=scale),
        in_specs=[VMEM_SPEC, VMEM_SPEC],
        out_specs=VMEM_SPEC,
        out_shape=jax.ShapeDtypeStruct((chans, lags * chans), jnp.float32),
        name=name,
    )(in_vmem(mod), in_vmem(other))


def gather_windows(whites, pairs, groups):
    white, for_start, for_both, for_end, for_late = whites
    windows, chans, width = white.shape
    total = windows * groups
    place = lax.axis_index("pair")
    at_start = place < 2
    alone = place == pairs - 2
    at_end = jnp.logical_and(place >= pairs - 4, jnp.logical_not(alone))
    single = pltpu.VMEM((total, chans, width), white.dtype)
    double = pltpu.VMEM((total, 2 * chans, width), white.dtype)

    def exchange(sends):
        return lax.all_to_all(sends, "tm", 0, 0, tiled=True)

    def one(block):
        return exchange(on_chip(spread_kernel, "spread", single, block))

    def both(white, far):
        return exchange(on_chip(slots_kernel, "slots", double, white, far))

    def after_own(far, own):
        return on_chip(merge_kernel, "merge", double, one(far), own)

    def put(kernel, name, block, gathered):
        return pl.pallas_call(
            kernel,
            in_specs=[VMEM_SPEC] * 2,
            out_specs=VMEM_SPEC,
            out_shape=double,
            input_output_aliases={1: 0},
            name=name,
        )(in_vmem(block), in_vmem(gathered))

    far = lax.ppermute(white, "pair", [(p, p - 2) for p in range(2, pairs - 2)])
    own = lax.cond(at_start, one, lambda white: unwritten(single.shape, single.dtype), for_start)
    white, own = lax.optimization_barrier((white, own))
    wrapped = lax.ppermute(
        white, "pair", [(p, (p - 2) % pairs) for p in (0, 1, pairs - 2, pairs - 1)]
    )
    own = lax.cond(alone, lambda block, own: one(block), lambda block, own: own, for_end, own)
    gathered = lax.switch(
        at_start.astype(jnp.int32) + 2 * alone.astype(jnp.int32) + 3 * at_end.astype(jnp.int32),
        (
            lambda for_both, far, own: both(for_both, far),
            lambda for_both, far, own: after_own(far, own),
            lambda for_both, far, own: on_chip(place_kernel, "place_own", double, own),
            lambda for_both, far, own: unwritten(double.shape, double.dtype),
        ),
        for_both,
        far,
        own,
    )
    return lax.switch(
        alone.astype(jnp.int32) + 2 * at_end.astype(jnp.int32),
        (
            lambda for_late, wrapped, gathered: gathered,
            lambda for_late, wrapped, gathered: put(
                put_far_kernel, "put_far", one(wrapped), gathered
            ),
            lambda for_late, wrapped, gathered: put(
                put_both_kernel, "put_both", both(for_late, wrapped), gathered
            ),
        ),
        for_late,
        wrapped,
        gathered,
    )


def local(raw, valid):
    windows, chans, samples = raw.shape
    freqs = samples // 2
    groups = lax.axis_size("tm")
    pairs = lax.axis_size("pair")
    total = windows * groups
    lags = LAGS // groups
    scale = 1.0 / math.sqrt(total * freqs)
    basis = jnp.asarray(make_basis(samples, freqs))
    table = jnp.asarray(lag_tables(LAGS, freqs, samples))
    whites = whiten(raw, valid, basis, 5)
    gathered = gather_windows(whites, pairs, groups)
    near = lax.ppermute(gathered[:, chans:, :], "pair", [(p, p ^ 1) for p in range(pairs)])
    far_corr, mod = correlate_far(gathered, table, lags, scale)
    near_corr = correlate(mod, near, lags, scale, "near_corr")
    return (near_corr, far_corr)


def solution(mesh):
    return jax.shard_map(
        local,
        mesh=mesh,
        in_specs=(P("tm", "pair", None), P("tm", "pair")),
        out_specs=(P("pair", "tm"), P("pair", "tm")),
        check_vma=False,
    )
```

```python
import functools
import math

import jax
import jax.numpy as jnp
import numpy as np
from jax import lax
from jax.experimental import pallas as pl
from jax.experimental.pallas import tpu as pltpu
from jax.sharding import PartitionSpec as P

LAGS = 16


def make_basis(samples, freqs):
    times = np.arange(samples, dtype=np.float64)[:, None]
    bins = np.arange(freqs, dtype=np.float64)[None, :]
    hann = 0.5 - 0.5 * np.cos(2.0 * math.pi * times / samples)
    angle = 2.0 * math.pi * bins * times / samples
    return np.concatenate([hann * np.cos(angle), -hann * np.sin(angle)], axis=1).astype(
        jnp.bfloat16
    )


def lag_tables(lags, freqs, samples):
    shift_lag = np.arange(lags, dtype=np.float64)[:, None] - lags // 2
    bins = np.arange(freqs, dtype=np.float64)[None, :]
    theta = 2.0 * math.pi * bins * shift_lag / samples
    cos = np.cos(theta).astype(jnp.bfloat16).astype(np.float32)
    sin = np.sin(theta).astype(jnp.bfloat16).astype(np.float32)
    return np.concatenate([cos, cos, -sin, sin], axis=1)


def in_vmem(value):
    return pltpu.with_memory_space_constraint(value, pltpu.VMEM)


VMEM_SPEC = pl.BlockSpec(memory_space=pltpu.VMEM)


def on_chip(kernel, name, out, *args):
    return pl.pallas_call(
        kernel,
        in_specs=[VMEM_SPEC] * len(args),
        out_specs=jax.tree.map(lambda _: VMEM_SPEC, out),
        out_shape=out,
        name=name,
    )(*[in_vmem(arg) for arg in args])


def whiten_kernel(raw_hbm, valid_hbm, basis_hbm, *refs):
    *white_refs, raw_ref, valid_ref, basis_ref, sems = refs
    moves = ((raw_hbm, raw_ref), (basis_hbm, basis_ref), (valid_hbm, valid_ref))
    loads = [pltpu.make_async_copy(src, dst, sems.at[i]) for i, (src, dst) in enumerate(moves)]
    for load in loads:
        load.start()
    for load in loads:
        load.wait()
    chans, width = white_refs[0].shape[1:]
    spectra = jnp.dot(raw_ref[0], basis_ref[...], preferred_element_type=jnp.float32)
    power = jnp.mean(spectra * spectra, axis=-1, keepdims=True) + 1e-06
    mask = jnp.transpose(jnp.broadcast_to(valid_ref[...].astype(jnp.float32), (width, chans)))
    white = (spectra * lax.rsqrt(power) * mask).astype(jnp.bfloat16)
    for white_ref in white_refs:
        white_ref[0] = white


def whiten(raw, valid, basis, copies):
    anywhere = pl.BlockSpec(memory_space=pl.ANY)
    return pl.pallas_call(
        whiten_kernel,
        in_specs=[anywhere] * 3,
        out_specs=[VMEM_SPEC] * copies,
        out_shape=[pltpu.VMEM(raw.shape, jnp.bfloat16)] * copies,
        scratch_shapes=[
            pltpu.VMEM(raw.shape, raw.dtype),
            pltpu.VMEM(valid.shape, valid.dtype),
            pltpu.VMEM(basis.shape, basis.dtype),
            pltpu.SemaphoreType.DMA((3,)),
        ],
        name="whiten",
    )(raw, valid, basis)


def slots_of(chans):
    odd = lax.axis_index("pair") & 1
    return pl.multiple_of(odd * chans, chans), pl.multiple_of((1 - odd) * chans, chans)


def slots_kernel(white_ref, far_ref, send_ref):
    peers, both, _ = send_ref.shape
    chans = both // 2
    own_at, far_at = slots_of(chans)
    for peer in range(peers):
        send_ref[peer, pl.ds(own_at, chans), :] = white_ref[0]
        send_ref[peer, pl.ds(far_at, chans), :] = far_ref[0]


def spread_kernel(block_ref, send_ref):
    for peer in range(send_ref.shape[0]):
        send_ref[peer] = block_ref[0]


def merge_kernel(far_ref, early_ref, gath_ref):
    chans = far_ref.shape[1]
    own_at, far_at = slots_of(chans)
    for w in range(far_ref.shape[0]):
        gath_ref[w, pl.ds(own_at, chans), :] = early_ref[w]
        gath_ref[w, pl.ds(far_at, chans), :] = far_ref[w]


def put_both_kernel(block_ref, old_ref, out_ref):
    del old_ref
    out_ref[...] = block_ref[...]


def unwritten(shape, dtype):
    return pl.pallas_call(
        lambda out_ref: None,
        out_specs=pl.BlockSpec(memory_space=pl.ANY),
        out_shape=jax.ShapeDtypeStruct(shape, dtype),
        name="unwritten",
    )()


def far_kernel(gath_ref, table_ref, out_hbm, mod_ref, out_ref, sems, *, scale):
    windows, both, width = gath_ref.shape
    chans = both // 2
    own_at, far_at = slots_of(chans)
    lags = mod_ref.shape[0] // chans
    other = jnp.concatenate(
        [gath_ref[w, pl.ds(far_at, chans), :] for w in range(windows)], axis=1
    )
    turns = [table_ref[pl.ds(lax.axis_index("tm") * lags + lag, 1), :] for lag in range(lags)]
    writes = []
    for lag, turn in enumerate(turns):
        rows = slice(lag * chans, (lag + 1) * chans)
        cos, sin = turn[:, :width], turn[:, width:]
        for w in range(windows):
            own = gath_ref[w, pl.ds(own_at, chans), :].astype(jnp.float32)
            turned = own * cos + pltpu.roll(own, width // 2, 1) * sin
            mod_ref[rows, w * width : (w + 1) * width] = turned.astype(jnp.bfloat16)
        total = lax.dot_general(
            mod_ref[rows, :], other, (((1,), (1,)), ((), ())), preferred_element_type=jnp.float32
        )
        out_ref[lag] = total * scale
        write = pltpu.make_async_copy(out_ref.at[lag], out_hbm.at[:, rows], sems.at[lag])
        write.start()
        writes.append(write)
    for write in writes:
        write.wait()


def correlate_far(gathered, table, lags, scale):
    windows, both, width = gathered.shape
    chans = both // 2
    return pl.pallas_call(
        functools.partial(far_kernel, scale=scale),
        in_specs=[VMEM_SPEC, VMEM_SPEC],
        out_specs=[pl.BlockSpec(memory_space=pl.ANY), VMEM_SPEC],
        out_shape=[
            jax.ShapeDtypeStruct((chans, lags * chans), jnp.float32),
            pltpu.VMEM((lags * chans, windows * width), jnp.bfloat16),
        ],
        scratch_shapes=[
            pltpu.VMEM((lags, chans, chans), jnp.float32),
            pltpu.SemaphoreType.DMA((lags,)),
        ],
        name="far_corr",
    )(in_vmem(gathered), in_vmem(table))


def corr_kernel(mod_ref, other_ref, out_ref, *, scale):
    windows, chans, _ = other_ref.shape
    other = jnp.concatenate([other_ref[w] for w in range(windows)], axis=1)
    total = lax.dot_general(
        mod_ref[...], other, (((1,), (1,)), ((), ())), preferred_element_type=jnp.float32
    )
    for lag in range(total.shape[0] // chans):
        rows = slice(lag * chans, (lag + 1) * chans)
        out_ref[:, rows] = total[rows] * scale


def correlate(mod, other, lags, scale, name):
    chans = other.shape[1]
    return pl.pallas_call(
        functools.partial(corr_kernel, scale=scale),
        in_specs=[VMEM_SPEC, VMEM_SPEC],
        out_specs=VMEM_SPEC,
        out_shape=jax.ShapeDtypeStruct((chans, lags * chans), jnp.float32),
        name=name,
    )(in_vmem(mod), in_vmem(other))


def gather_windows(whites, pairs, groups):
    white, for_start, for_both, for_late = whites
    windows, chans, width = white.shape
    total = windows * groups
    place = lax.axis_index("pair")
    at_start = place < 2
    at_end = place >= pairs - 4
    single = pltpu.VMEM((total, chans, width), white.dtype)
    double = pltpu.VMEM((total, 2 * chans, width), white.dtype)

    def exchange(sends):
        return lax.all_to_all(sends, "tm", 0, 0, tiled=True)

    def one(block):
        return exchange(on_chip(spread_kernel, "spread", single, block))

    def both(white, far):
        return exchange(on_chip(slots_kernel, "slots", double, white, far))

    def after_own(far, own):
        return on_chip(merge_kernel, "merge", double, one(far), own)

    def put(block, gathered):
        return pl.pallas_call(
            put_both_kernel,
            in_specs=[VMEM_SPEC] * 2,
            out_specs=VMEM_SPEC,
            out_shape=double,
            input_output_aliases={1: 0},
            name="put_both",
        )(in_vmem(block), in_vmem(gathered))

    far = lax.ppermute(white, "pair", [(p, p - 2) for p in range(2, pairs - 2)])
    own = lax.cond(at_start, one, lambda white: unwritten(single.shape, single.dtype), for_start)
    white, own = lax.optimization_barrier((white, own))
    wrapped = lax.ppermute(
        white, "pair", [(p, (p - 2) % pairs) for p in (0, 1, pairs - 2, pairs - 1)]
    )
    gathered = lax.switch(
        at_start.astype(jnp.int32) + 2 * at_end.astype(jnp.int32),
        (
            lambda for_both, far, own: both(for_both, far),
            lambda for_both, far, own: after_own(far, own),
            lambda for_both, far, own: unwritten(double.shape, double.dtype),
        ),
        for_both,
        far,
        own,
    )
    return lax.cond(
        at_end,
        lambda for_late, wrapped, gathered: put(both(for_late, wrapped), gathered),
        lambda for_late, wrapped, gathered: gathered,
        for_late,
        wrapped,
        gathered,
    )


def local(raw, valid):
    windows, chans, samples = raw.shape
    freqs = samples // 2
    groups = lax.axis_size("tm")
    pairs = lax.axis_size("pair")
    total = windows * groups
    lags = LAGS // groups
    scale = 1.0 / math.sqrt(total * freqs)
    basis = jnp.asarray(make_basis(samples, freqs))
    table = jnp.asarray(lag_tables(LAGS, freqs, samples))
    whites = whiten(raw, valid, basis, 4)
    gathered = gather_windows(whites, pairs, groups)
    near = lax.ppermute(gathered[:, chans:, :], "pair", [(p, p ^ 1) for p in range(pairs)])
    far_corr, mod = correlate_far(gathered, table, lags, scale)
    near_corr = correlate(mod, near, lags, scale, "near_corr")
    return (near_corr, far_corr)


def solution(mesh):
    return jax.shard_map(
        local,
        mesh=mesh,
        in_specs=(P("tm", "pair", None), P("tm", "pair")),
        out_specs=(P("pair", "tm"), P("pair", "tm")),
        check_vma=False,
    )
```

```python
import functools
import math

import jax
import jax.numpy as jnp
import numpy as np
from jax import lax
from jax.experimental import pallas as pl
from jax.experimental.pallas import tpu as pltpu
from jax.sharding import PartitionSpec as P

LAGS = 16


def make_basis(samples, freqs):
    times = np.arange(samples, dtype=np.float64)[:, None]
    bins = np.arange(freqs, dtype=np.float64)[None, :]
    hann = 0.5 - 0.5 * np.cos(2.0 * math.pi * times / samples)
    angle = 2.0 * math.pi * bins * times / samples
    return np.concatenate([hann * np.cos(angle), -hann * np.sin(angle)], axis=1).astype(
        jnp.bfloat16
    )


def lag_tables(lags, freqs, samples):
    shift_lag = np.arange(lags, dtype=np.float64)[:, None] - lags // 2
    bins = np.arange(freqs, dtype=np.float64)[None, :]
    theta = 2.0 * math.pi * bins * shift_lag / samples
    cos = np.cos(theta).astype(jnp.bfloat16).astype(np.float32)
    sin = np.sin(theta).astype(jnp.bfloat16).astype(np.float32)
    return np.concatenate([cos, cos, -sin, sin], axis=1)


def in_vmem(value):
    return pltpu.with_memory_space_constraint(value, pltpu.VMEM)


VMEM_SPEC = pl.BlockSpec(memory_space=pltpu.VMEM)


def on_chip(kernel, name, out, *args):
    return pl.pallas_call(
        kernel,
        in_specs=[VMEM_SPEC] * len(args),
        out_specs=jax.tree.map(lambda _: VMEM_SPEC, out),
        out_shape=out,
        name=name,
    )(*[in_vmem(arg) for arg in args])


def whiten_kernel(raw_hbm, valid_hbm, basis_hbm, *refs):
    *white_refs, raw_ref, valid_ref, basis_ref, sems = refs
    moves = ((raw_hbm, raw_ref), (basis_hbm, basis_ref), (valid_hbm, valid_ref))
    loads = [pltpu.make_async_copy(src, dst, sems.at[i]) for i, (src, dst) in enumerate(moves)]
    for load in loads:
        load.start()
    for load in loads:
        load.wait()
    chans, width = white_refs[0].shape[1:]
    spectra = jnp.dot(raw_ref[0], basis_ref[...], preferred_element_type=jnp.float32)
    power = jnp.mean(spectra * spectra, axis=-1, keepdims=True) + 1e-06
    mask = jnp.transpose(jnp.broadcast_to(valid_ref[...].astype(jnp.float32), (width, chans)))
    white = (spectra * lax.rsqrt(power) * mask).astype(jnp.bfloat16)
    for white_ref in white_refs:
        white_ref[0] = white


def whiten(raw, valid, basis, copies):
    anywhere = pl.BlockSpec(memory_space=pl.ANY)
    return pl.pallas_call(
        whiten_kernel,
        in_specs=[anywhere] * 3,
        out_specs=[VMEM_SPEC] * copies,
        out_shape=[pltpu.VMEM(raw.shape, jnp.bfloat16)] * copies,
        scratch_shapes=[
            pltpu.VMEM(raw.shape, raw.dtype),
            pltpu.VMEM(valid.shape, valid.dtype),
            pltpu.VMEM(basis.shape, basis.dtype),
            pltpu.SemaphoreType.DMA((3,)),
        ],
        name="whiten",
    )(raw, valid, basis)


def slots_of(chans):
    odd = lax.axis_index("pair") & 1
    return pl.multiple_of(odd * chans, chans), pl.multiple_of((1 - odd) * chans, chans)


def slots_kernel(white_ref, far_ref, send_ref):
    peers, both, _ = send_ref.shape
    chans = both // 2
    own_at, far_at = slots_of(chans)
    for peer in range(peers):
        send_ref[peer, pl.ds(own_at, chans), :] = white_ref[0]
        send_ref[peer, pl.ds(far_at, chans), :] = far_ref[0]


def spread_kernel(block_ref, send_ref):
    for peer in range(send_ref.shape[0]):
        send_ref[peer] = block_ref[0]


def merge_kernel(far_ref, early_ref, gath_ref):
    chans = far_ref.shape[1]
    own_at, far_at = slots_of(chans)
    for w in range(far_ref.shape[0]):
        gath_ref[w, pl.ds(own_at, chans), :] = early_ref[w]
        gath_ref[w, pl.ds(far_at, chans), :] = far_ref[w]


def put_both_kernel(block_ref, old_ref, out_ref):
    del old_ref
    out_ref[...] = block_ref[...]


def unwritten(shape, dtype):
    return pl.pallas_call(
        lambda out_ref: None,
        out_specs=pl.BlockSpec(memory_space=pl.ANY),
        out_shape=jax.ShapeDtypeStruct(shape, dtype),
        name="unwritten",
    )()


def far_kernel(gath_ref, table_ref, out_hbm, mod_ref, out_ref, sems, *, scale):
    windows, both, width = gath_ref.shape
    chans = both // 2
    own_at, far_at = slots_of(chans)
    lags = mod_ref.shape[0] // chans
    other = jnp.concatenate(
        [gath_ref[w, pl.ds(far_at, chans), :] for w in range(windows)], axis=1
    )
    turns = [table_ref[pl.ds(lax.axis_index("tm") * lags + lag, 1), :] for lag in range(lags)]
    writes = []
    for lag, turn in enumerate(turns):
        rows = slice(lag * chans, (lag + 1) * chans)
        cos, sin = turn[:, :width], turn[:, width:]
        for w in range(windows):
            own = gath_ref[w, pl.ds(own_at, chans), :].astype(jnp.float32)
            turned = own * cos + pltpu.roll(own, width // 2, 1) * sin
            mod_ref[rows, w * width : (w + 1) * width] = turned.astype(jnp.bfloat16)
        total = lax.dot_general(
            mod_ref[rows, :], other, (((1,), (1,)), ((), ())), preferred_element_type=jnp.float32
        )
        out_ref[lag] = total * scale
        write = pltpu.make_async_copy(out_ref.at[lag], out_hbm.at[:, rows], sems.at[lag])
        write.start()
        writes.append(write)
    for write in writes:
        write.wait()


def correlate_far(gathered, table, lags, scale):
    windows, both, width = gathered.shape
    chans = both // 2
    return pl.pallas_call(
        functools.partial(far_kernel, scale=scale),
        in_specs=[VMEM_SPEC, VMEM_SPEC],
        out_specs=[pl.BlockSpec(memory_space=pl.ANY), VMEM_SPEC],
        out_shape=[
            jax.ShapeDtypeStruct((chans, lags * chans), jnp.float32),
            pltpu.VMEM((lags * chans, windows * width), jnp.bfloat16),
        ],
        scratch_shapes=[
            pltpu.VMEM((lags, chans, chans), jnp.float32),
            pltpu.SemaphoreType.DMA((lags,)),
        ],
        name="far_corr",
    )(in_vmem(gathered), in_vmem(table))


def corr_kernel(mod_ref, other_ref, out_hbm, out_ref, sems, *, scale):
    windows, chans, _ = other_ref.shape
    other = jnp.concatenate([other_ref[w] for w in range(windows)], axis=1)
    total = lax.dot_general(
        mod_ref[...], other, (((1,), (1,)), ((), ())), preferred_element_type=jnp.float32
    )
    writes = []
    for lag in range(total.shape[0] // chans):
        rows = slice(lag * chans, (lag + 1) * chans)
        out_ref[lag] = total[rows] * scale
        write = pltpu.make_async_copy(out_ref.at[lag], out_hbm.at[:, rows], sems.at[lag])
        write.start()
        writes.append(write)
    for write in writes:
        write.wait()


def correlate(mod, other, lags, scale, name):
    chans = other.shape[1]
    return pl.pallas_call(
        functools.partial(corr_kernel, scale=scale),
        in_specs=[VMEM_SPEC, VMEM_SPEC],
        out_specs=pl.BlockSpec(memory_space=pl.ANY),
        out_shape=jax.ShapeDtypeStruct((chans, lags * chans), jnp.float32),
        scratch_shapes=[
            pltpu.VMEM((lags, chans, chans), jnp.float32),
            pltpu.SemaphoreType.DMA((lags,)),
        ],
        name=name,
    )(in_vmem(mod), in_vmem(other))


def gather_windows(whites, pairs, groups):
    white, for_start, for_both, for_late = whites
    windows, chans, width = white.shape
    total = windows * groups
    place = lax.axis_index("pair")
    at_start = place < 2
    at_end = place >= pairs - 4
    single = pltpu.VMEM((total, chans, width), white.dtype)
    double = pltpu.VMEM((total, 2 * chans, width), white.dtype)

    def exchange(sends):
        return lax.all_to_all(sends, "tm", 0, 0, tiled=True)

    def one(block):
        return exchange(on_chip(spread_kernel, "spread", single, block))

    def both(white, far):
        return exchange(on_chip(slots_kernel, "slots", double, white, far))

    def after_own(far, own):
        return on_chip(merge_kernel, "merge", double, one(far), own)

    def put(block, gathered):
        return pl.pallas_call(
            put_both_kernel,
            in_specs=[VMEM_SPEC] * 2,
            out_specs=VMEM_SPEC,
            out_shape=double,
            input_output_aliases={1: 0},
            name="put_both",
        )(in_vmem(block), in_vmem(gathered))

    far = lax.ppermute(white, "pair", [(p, p - 2) for p in range(2, pairs - 2)])
    own = lax.cond(at_start, one, lambda white: unwritten(single.shape, single.dtype), for_start)
    white, own = lax.optimization_barrier((white, own))
    wrapped = lax.ppermute(
        white, "pair", [(p, (p - 2) % pairs) for p in (0, 1, pairs - 2, pairs - 1)]
    )
    gathered = lax.switch(
        at_start.astype(jnp.int32) + 2 * at_end.astype(jnp.int32),
        (
            lambda for_both, far, own: both(for_both, far),
            lambda for_both, far, own: after_own(far, own),
            lambda for_both, far, own: unwritten(double.shape, double.dtype),
        ),
        for_both,
        far,
        own,
    )
    return lax.cond(
        at_end,
        lambda for_late, wrapped, gathered: put(both(for_late, wrapped), gathered),
        lambda for_late, wrapped, gathered: gathered,
        for_late,
        wrapped,
        gathered,
    )


def local(raw, valid):
    windows, chans, samples = raw.shape
    freqs = samples // 2
    groups = lax.axis_size("tm")
    pairs = lax.axis_size("pair")
    total = windows * groups
    lags = LAGS // groups
    scale = 1.0 / math.sqrt(total * freqs)
    basis = jnp.asarray(make_basis(samples, freqs))
    table = jnp.asarray(lag_tables(LAGS, freqs, samples))
    whites = whiten(raw, valid, basis, 4)
    gathered = gather_windows(whites, pairs, groups)
    near = lax.ppermute(gathered[:, chans:, :], "pair", [(p, p ^ 1) for p in range(pairs)])
    far_corr, mod = correlate_far(gathered, table, lags, scale)
    near_corr = correlate(mod, near, lags, scale, "near_corr")
    return (near_corr, far_corr)


def solution(mesh):
    return jax.shard_map(
        local,
        mesh=mesh,
        in_specs=(P("tm", "pair", None), P("tm", "pair")),
        out_specs=(P("pair", "tm"), P("pair", "tm")),
        check_vma=False,
    )
```
